32 devices in a mesh: ctx: 8 (over z, y), head: 4 (over x, core).
Axes of the slice: x: 2, y: 2, z: 4, core: 2. Of those that a mesh axis runs over, the one named last changes fastest.
Arguments:
- token_queries: bfloat16 [2048, 8192], P(('ctx', 'head')), may hold values from -4.5 to 4.5
- token_keys: bfloat16 [2048, 1024], P(('ctx', 'head')), may hold values from -4.5 to 4.5
- token_values: bfloat16 [2048, 1024], P(('ctx', 'head')), may hold values from -6 to 6
- doc_lengths: int32 [4], replicated, may hold values from 1 to 1024, 2048 in all
Outputs:
- attended: bfloat16 [2048, 8192], P(('ctx', 'head'))
The draws below stay inside these ranges and needn't reach their ends.
Inputs may be any that keep to these rules, and one draw needn't show every extreme that they name: `doc_lengths`: the lengths sum to 2048; the longest is exactly 1024.
All inputs are finite; a program needn't handle non-finite values.
Results may differ from the reference program's by a relative error of at most 0.0035.
Values may be sent and summed in bfloat16 or wider, within the bound.
No kernel may reach another device: no remote copies, remote signals or barrier semaphores. Data moves between devices by JAX's collectives and lax.ppermute only.
A program may use at most 64 MiB of HBM per device.

```python
import math
import jax
import jax.numpy as jnp
import numpy as np
from jax import lax

QUERY_HEADS = 64
KEY_VALUE_HEADS = 8
HEAD_SIZE = 128
PACKED_TOKENS = 2048
LONGEST_TOKENS = 1024
DOCS = 4


def draw_token_queries(key, part):
    return jnp.clip(jax.random.normal(jax.random.fold_in(key, 22), (PACKED_TOKENS, QUERY_HEADS * HEAD_SIZE), jnp.float32), -4.5, 4.5).astype(jnp.bfloat16)


def draw_token_keys(key, part):
    return jnp.clip(jax.random.normal(jax.random.fold_in(key, 32), (PACKED_TOKENS, KEY_VALUE_HEADS * HEAD_SIZE), jnp.float32), -4.5, 4.5).astype(jnp.bfloat16)


def shard_levels(key, extent, cuts, least, high):
    loudness = 1.0
    for dim, shards_of in cuts:
        steps = jax.random.uniform(jax.random.fold_in(jax.random.fold_in(key, 6), dim), (shards_of,), jnp.float32, least / len(cuts), high / len(cuts))
        loudness = loudness * jnp.repeat(jnp.exp(steps), extent[dim] // shards_of).reshape((-1,) + (1,) * (len(extent) - 1 - dim))
    return loudness


def profile(count, total, reach, skew):
    loads = [(1 << 20) // math.isqrt(standing ** skew) + 1 for standing in range(2, count + 1)]
    spare, counts = total - reach - (count - 1), [1] * (count - 1)
    while spare > 0:
        free = [i for i in range(count - 1) if counts[i] < reach]
        whole, left = sum([loads[i] for i in free]), spare
        for i in free:
            extra = min(reach - counts[i], max(1, left * loads[i] // whole), spare)
            counts[i] = counts[i] + extra
            spare = spare - extra
    return np.array([reach] + counts)


def uneven(own_key, amount, total, limit, lean):
    if amount == 2:
        one = jax.random.randint(own_key, (), max(1, total - limit), min(limit, total - 1) + 1)
        return jnp.stack([one, total - one])
    tallies = jnp.asarray(profile(amount, total, limit, lean), jnp.int32)
    twos = (amount - 1) // 2
    source_of, receiver = tallies[1:1 + 2 * twos:2], tallies[2:2 + 2 * twos:2]
    room = jnp.minimum(source_of - 1, limit - receiver)
    shifted = jax.random.randint(jax.random.fold_in(own_key, 1), (twos,), 0, 1 << 20) % (room + 1)
    tallies = tallies.at[1:1 + 2 * twos:2].set(source_of - shifted).at[2:2 + 2 * twos:2].set(receiver + shifted)
    return tallies[jax.random.permutation(jax.random.fold_in(own_key, 2), amount)]


def centred(key, shape, width, limit, cuts=(), held_as=jnp.bfloat16):
    loudness = shard_levels(key, shape, cuts, -0.22, 0.18) if cuts else 1.0
    values = jax.random.normal(key, shape, jnp.float32) * width * loudness
    return jnp.minimum(jnp.maximum(values, -limit), limit).astype(held_as)


def setup_inputs(seed: int = 0) -> dict:
    seeds = jax.random.split(jax.random.key(seed), 5)
    token_queries = draw_token_queries(jax.random.fold_in(seeds[4], 71), 0)
    token_keys = draw_token_keys(jax.random.fold_in(seeds[4], 71), 0)
    token_values = centred(seeds[2], (PACKED_TOKENS, KEY_VALUE_HEADS * HEAD_SIZE), 1.0, 6.0, ((0, 32),))
    doc_lengths = uneven(seeds[3], DOCS, PACKED_TOKENS, LONGEST_TOKENS, 2).astype(jnp.int32)
    return dict(token_queries=token_queries, token_keys=token_keys, token_values=token_values, doc_lengths=doc_lengths)


def document_index(positions, bounds):
    return jnp.sum((bounds[None, :] <= positions[:, None]).astype(jnp.int32), axis=1)


def reference(token_queries, token_keys, token_values, doc_lengths):
    negative_big = -1e30
    bounds = jnp.cumsum(doc_lengths).astype(jnp.int32)
    positions = jnp.arange(PACKED_TOKENS, dtype=jnp.int32)
    documents = document_index(positions, bounds)
    group_factor = QUERY_HEADS // KEY_VALUE_HEADS
    query_matrix = token_queries.reshape(PACKED_TOKENS, KEY_VALUE_HEADS, group_factor, HEAD_SIZE).astype(jnp.float32)
    padding_amount = jnp.zeros((LONGEST_TOKENS, KEY_VALUE_HEADS, HEAD_SIZE), jnp.float32)
    keys_padded = jnp.concatenate([padding_amount, token_keys.reshape(PACKED_TOKENS, KEY_VALUE_HEADS, HEAD_SIZE).astype(jnp.float32)], axis=0)
    values_padded = jnp.concatenate([padding_amount, token_values.reshape(PACKED_TOKENS, KEY_VALUE_HEADS, HEAD_SIZE).astype(jnp.float32)], axis=0)
    padded_docs = jnp.concatenate([jnp.full((LONGEST_TOKENS,), -1, jnp.int32), documents], axis=0)
    padded_pos = jnp.concatenate([jnp.arange(LONGEST_TOKENS, dtype=jnp.int32) - LONGEST_TOKENS, positions], axis=0)
    block_rows = math.gcd(PACKED_TOKENS, 256)
    window = LONGEST_TOKENS + block_rows
    score_scale = HEAD_SIZE ** -0.5

    def one_block(block_index):
        offset = (block_index * block_rows).astype(jnp.int32)
        query_block = lax.dynamic_slice_in_dim(query_matrix, offset, block_rows, 0)
        query_docs = lax.dynamic_slice_in_dim(documents, offset, block_rows, 0)
        query_pos = lax.dynamic_slice_in_dim(positions, offset, block_rows, 0)
        key_block = lax.dynamic_slice_in_dim(keys_padded, offset, window, 0)
        value_block = lax.dynamic_slice_in_dim(values_padded, offset, window, 0)
        key_docs = lax.dynamic_slice_in_dim(padded_docs, offset, window, 0)
        key_pos = lax.dynamic_slice_in_dim(padded_pos, offset, window, 0)
        scores = jnp.einsum('qgrd,kgd->qgrk', query_block, key_block, precision=lax.Precision.HIGHEST) * score_scale
        allowed = (query_docs[:, None] == key_docs[None, :]) & (key_pos[None, :] <= query_pos[:, None])
        allowed = allowed[:, None, None, :]
        masked = jnp.where(allowed, scores, negative_big)
        row_max = jnp.max(masked, axis=-1, keepdims=True)
        weights = jnp.where(allowed, jnp.exp(masked - row_max), 0.0)
        weight_sum = jnp.sum(weights, axis=-1)
        rounded = lax.optimization_barrier(weights.astype(jnp.bfloat16)).astype(jnp.float32)
        combined = jnp.einsum('qgrk,kgd->qgrd', rounded, value_block, precision=lax.Precision.HIGHEST)
        return (combined / weight_sum[..., None]).reshape(block_rows, QUERY_HEADS * HEAD_SIZE).astype(jnp.bfloat16)

    blocks_out = lax.map(one_block, jnp.arange(PACKED_TOKENS // block_rows, dtype=jnp.int32))
    return blocks_out.reshape(PACKED_TOKENS, QUERY_HEADS * HEAD_SIZE)
```

```python
import functools

import jax
import jax.numpy as jnp
import numpy as np
from jax import lax
from jax.experimental import pallas as pl
from jax.experimental.pallas import tpu as pltpu
from jax.sharding import PartitionSpec as P

QUERY_HEADS = 64
KEY_VALUE_HEADS = 8
HEAD_SIZE = 128
GROUP = QUERY_HEADS // KEY_VALUE_HEADS
CORES = 2
NEGATIVE_BIG = -1e30
LOG2_SCALE = HEAD_SIZE ** (-0.5) * float(np.log2(np.e))
AXES = ("ctx", "head")


def attend_kernel(blocks, first, last, base_ref, edges_ref, q_ref, *refs):
    block_refs, refs = refs[:blocks], refs[blocks:]
    if not first:
        (mean_ref, level_ref), refs = refs[:2], refs[2:]
    if last:
        out_ref, refs = refs[0], refs[1:]
    else:
        (mean_out, level_out), refs = refs[:2], refs[2:]
    key_marks, query_marks = refs
    tokens = q_ref.shape[0]
    rows = tokens * GROUP

    @pl.when(pl.program_id(0) == 0)
    def _():
        low, high = edges_ref[0:1, :], edges_ref[1:2, :]
        inside = lax.broadcasted_iota(jnp.int32, (tokens, HEAD_SIZE), 0)
        for i in range(blocks):
            position = base_ref[i + 1] + inside
            other = (position < low) | (position >= high)
            key_marks[i * tokens:(i + 1) * tokens, :] = jnp.where(other, NEGATIVE_BIG, 0.0).astype(jnp.bfloat16)
        position = base_ref[0] + inside
        own = (position >= low) & (position < high)
        query_marks[...] = jnp.where(own, 1.0, 0.0).astype(jnp.bfloat16)

    marks = query_marks[...]
    queries = jnp.concatenate(
        [
            jnp.concatenate([q_ref[:, r * HEAD_SIZE:(r + 1) * HEAD_SIZE], marks], axis=1)
            for r in range(GROUP)
        ],
        axis=0,
    )
    keys = jnp.concatenate([block[0:tokens, :] for block in block_refs], axis=0)
    keys = jnp.concatenate([keys, key_marks[...]], axis=1)
    values = jnp.concatenate([block[tokens:, :] for block in block_refs], axis=0)
    values = jnp.concatenate([values, jnp.ones_like(values)], axis=1)
    scores = lax.dot_general(
        queries, keys, (((1,), (1,)), ((), ())), preferred_element_type=jnp.float32
    )
    if first:
        token = lax.broadcasted_iota(jnp.int32, scores.shape, 0) % tokens
        column = lax.broadcasted_iota(jnp.int32, scores.shape, 1)
        scores = jnp.where((column > token) & (column < tokens), NEGATIVE_BIG, scores)
    top = jnp.max(scores, axis=1, keepdims=True) * LOG2_SCALE
    if not first:
        top = jnp.maximum(top, level_ref[:, 0:1])
    weights = jnp.exp2(scores * LOG2_SCALE - top).astype(jnp.bfloat16)
    summed = jnp.dot(weights, values, preferred_element_type=jnp.float32)
    weighted, weight_sum = summed[:, :HEAD_SIZE], summed[:, HEAD_SIZE:]
    if not first:
        share = jnp.exp2(level_ref[...] - top)
        weighted = weighted + share * mean_ref[...]
        weight_sum = weight_sum + share
    mean = weighted / weight_sum
    if last:
        for r in range(GROUP):
            out_ref[:, r * HEAD_SIZE:(r + 1) * HEAD_SIZE] = mean[r * tokens:(r + 1) * tokens].astype(out_ref.dtype)
    else:
        mean_out[...] = mean
        level_out[...] = top + jnp.log2(weight_sum)


def attend(queries, base, edges, blocks, state, last):
    tokens = queries.shape[0]
    rows = tokens * GROUP
    wide = pl.BlockSpec((tokens, GROUP * HEAD_SIZE), lambda g, *_: (0, g))
    tall = pl.BlockSpec((rows, HEAD_SIZE), lambda g, *_: (g, 0))
    pair = pl.BlockSpec((2 * tokens, HEAD_SIZE), lambda g, *_: (0, g))
    whole = pl.BlockSpec(edges.shape, lambda g, *_: (0, 0))
    carried = jax.ShapeDtypeStruct((KEY_VALUE_HEADS * rows, HEAD_SIZE), jnp.float32)
    keys = len(blocks) * tokens
    return pl.pallas_call(
        functools.partial(attend_kernel, len(blocks), state is None, last),
        out_shape=jax.ShapeDtypeStruct(queries.shape, queries.dtype) if last else (carried, carried),
        grid_spec=pltpu.PrefetchScalarGridSpec(
            num_scalar_prefetch=1,
            grid=(KEY_VALUE_HEADS,),
            in_specs=[whole, wide] + [pair] * len(blocks) + ([] if state is None else [tall, tall]),
            out_specs=wide if last else (tall, tall),
            scratch_shapes=[
                pltpu.VMEM((keys, HEAD_SIZE), jnp.bfloat16),
                pltpu.VMEM((tokens, HEAD_SIZE), jnp.bfloat16),
            ],
        ),
        cost_estimate=pl.CostEstimate(
            flops=8 * KEY_VALUE_HEADS * rows * keys * HEAD_SIZE,
            transcendentals=KEY_VALUE_HEADS * rows * keys,
            bytes_accessed=keys * 4096 + 4 * queries.size,
        ),
    )(base, edges, queries, *blocks, *(state or ()))


def on_device(sizes, token_queries, token_keys, token_values, doc_lengths):
    ctx, head = sizes
    side = head // CORES
    planes = ctx // side
    reach = planes // 2
    tokens = token_queries.shape[0]

    def shifted(dz, along):
        pairs = []
        for z in range(planes):
            for y in range(side):
                for x in range(side):
                    for core in range(CORES):
                        place = [y, x]
                        if along is not None:
                            which = 1 - along if core == 0 else along
                            place[which] = (place[which] + 1) % side
                        up = (z + dz) % planes
                        pairs.append(
                            (((z * side + y) * side + x) * CORES + core, ((up * side + place[0]) * side + place[1]) * CORES + core)
                        )
        return pairs

    def send(value, dz=0, along=None):
        return lax.ppermute(value, AXES, shifted(dz, along))

    def partner(value):
        return lax.ppermute(value, "head", [(h, h ^ 1) for h in range(head)])

    bounds = jnp.cumsum(doc_lengths)
    docs = doc_lengths.shape[0]
    edges = jnp.zeros((8, HEAD_SIZE), jnp.int32)
    edges = edges.at[1, :docs].set(bounds).at[0, 1:docs].set(bounds[:-1])

    h = lax.axis_index("head")
    c = lax.axis_index("ctx")
    z, y, x, core = c // side, c % side, h // CORES, h % CORES
    own_base = ((z * side + y) * side + x) * CORES * tokens + core * tokens

    def bases(hops):
        order = [(a, b, s) for s in range(CORES) for a in range(side) for b in range(side)]
        a, b, s = (jnp.asarray(np.array(v, np.int32)) for v in zip(*order))
        lane = core ^ s
        dx, dy = jnp.where(lane == 0, a, b), jnp.where(lane == 0, b, a)
        from_x, from_y = (x - dx) % side, (y - dy) % side
        base = ((((z - hops) * side + from_y) * side + from_x) * CORES + lane) * tokens
        return jnp.where((base <= own_base) & (z >= hops), base, -(1 << 24))

    def gathered(value):
        grid = [[None] * side for _ in range(side)]
        grid[0][0] = value
        for a in range(1, side):
            grid[a][0] = send(grid[a - 1][0], along=0)
        for a in range(side):
            for b in range(1, side):
                grid[a][b] = send(grid[a][b - 1], along=1)
        mine = [v for row in grid for v in row]
        return mine + [partner(v) for v in mine]

    own = jnp.concatenate([token_keys, token_values], axis=0)
    travelling, state = own, None
    layers = [own]
    for hop in range(reach):
        layers.append(send(layers[-1], dz=1))
    for hop, layer in enumerate(layers):
        base = jnp.concatenate([own_base[None], bases(hop)])
        state = attend(token_queries, base, edges, gathered(layer), state, hop == reach)
    return state


def solution(mesh):
    spec = P(AXES, None)
    return jax.shard_map(
        functools.partial(on_device, (mesh.shape["ctx"], mesh.shape["head"])),
        mesh=mesh, in_specs=(spec, spec, spec, P()), out_specs=spec, check_vma=False,
    )
```

```python
import functools

import jax
import jax.numpy as jnp
import numpy as np
from jax import lax
from jax.experimental import pallas as pl
from jax.experimental.pallas import tpu as pltpu
from jax.sharding import PartitionSpec as P

QUERY_HEADS = 64
KEY_VALUE_HEADS = 8
HEAD_SIZE = 128
GROUP = QUERY_HEADS // KEY_VALUE_HEADS
CORES = 2
NEGATIVE_BIG = -1e30
LOG2_SCALE = HEAD_SIZE ** (-0.5) * float(np.log2(np.e))
SUM_LEAST, SUM_MOST = 2.0**-60, 2.0**100
FAR = 1 << 30
AXES = ("ctx", "head")
LANES = 128


def columns(index):
    return pl.ds(pl.multiple_of(index * HEAD_SIZE, HEAD_SIZE), HEAD_SIZE)


def place(side):
    c, h = lax.axis_index("ctx"), lax.axis_index("head")
    return c // side, c % side, h // CORES, h % CORES


def mark_edges(doc_ref, tokens):
    lane = lax.broadcasted_iota(jnp.int32, (1, LANES), 1)
    low = jnp.where(lane >= LANES - tokens, -FAR, 0)
    high = jnp.where(lane >= LANES - tokens, FAR, 0)
    start = jnp.int32(0)
    for d in range(doc_ref.shape[0]):
        stop = start + doc_ref[d]
        low = jnp.where(lane == d, start, low)
        high = jnp.where(lane == d, stop, high)
        start = stop
    return low, high


def mark_keys(doc_ref, marks_ref, side, tokens, hops):
    low, high = mark_edges(doc_ref, tokens)
    z, y, x, core = place(side)
    inside = lax.broadcasted_iota(jnp.int32, (tokens, LANES), 0)
    lane = lax.broadcasted_iota(jnp.int32, (tokens, LANES), 1)
    own_base = (((z * side + y) * side + x) * CORES + core) * tokens
    index = 0
    for other_core in range(CORES):
        on = core ^ other_core
        for a in range(side):
            for b in range(side):
                dx, dy = jnp.where(on == 0, a, b), jnp.where(on == 0, b, a)
                from_x, from_y = lax.rem(x - dx + side, side), lax.rem(y - dy + side, side)
                base = ((((z - hops) * side + from_y) * side + from_x) * CORES + on) * tokens
                base = jnp.where((z >= hops) & (base <= own_base), base, -(FAR >> 1))
                position = base + inside
                hidden = (position < low) | (position >= high)
                if hops == 0 and index == 0:
                    hidden |= (lane >= LANES - tokens) & (lane - (LANES - tokens) < inside)
                marks_ref[index * tokens:(index + 1) * tokens, :] = jnp.where(hidden, NEGATIVE_BIG, 0.0).astype(
                    marks_ref.dtype
                )
                index += 1


def mark_queries(doc_ref, marks_ref, side, tokens):
    low, high = mark_edges(doc_ref, tokens)
    z, y, x, core = place(side)
    own_base = (((z * side + y) * side + x) * CORES + core) * tokens
    inside = lax.broadcasted_iota(jnp.int32, (tokens, LANES), 0)
    lane = lax.broadcasted_iota(jnp.int32, (tokens, LANES), 1)
    position = own_base + inside
    one = (lane - (LANES - tokens) == inside) | ((position >= low) & (position < high) & (lane < LANES - tokens))
    marks_ref[...] = jnp.where(one, 1.0, 0.0).astype(marks_ref.dtype)


def all_queries(q_ref, marks_ref, group):
    marks = marks_ref[...]
    return jnp.concatenate(
        [jnp.concatenate([q_ref[:, columns(group * GROUP + r)], marks], axis=1) for r in range(GROUP)], axis=0
    )


def all_keys(block_refs, marks_ref, tokens, group):
    keys = jnp.concatenate([block[:tokens, columns(group)] for block in block_refs], axis=0)
    return jnp.concatenate([keys, marks_ref[...]], axis=1)


def all_values(block_refs, tokens, group):
    values = jnp.concatenate([block[tokens:, columns(group)] for block in block_refs], axis=0)
    return jnp.concatenate([values, jnp.ones_like(values)], axis=1)


def scores_of(queries, keys):
    return lax.dot_general(queries, keys, (((1,), (1,)), ((), ())), preferred_element_type=jnp.float32)


def plane_kernel(side, hops, last, doc_ref, q_ref, *refs):
    planes = hops + 1 if last else 1
    per_plane = CORES * side * side
    blocks, refs = refs[:planes * per_plane], refs[planes * per_plane:]
    planes_of = [blocks[i * per_plane:(i + 1) * per_plane] for i in range(planes)]
    tokens = q_ref.shape[0]
    rows = tokens * GROUP
    if hops:
        running, refs = refs[0], refs[1:]
    result, key_marks, query_marks = refs[:3]
    mark_queries(doc_ref, query_marks, side, tokens)
    mark_keys(doc_ref, key_marks, side, tokens, hops)
    if last:
        staged, least, most, sem = refs[3:]
        least[...] = jnp.full(least.shape, SUM_MOST, jnp.float32)
        most[...] = jnp.full(most.shape, SUM_LEAST, jnp.float32)

    def write(group, mean):
        for r in range(GROUP):
            staged[:, columns(group * GROUP + r)] = mean[r * tokens:(r + 1) * tokens].astype(staged.dtype)

    def sent(group):
        part = pl.ds(pl.multiple_of(group * GROUP * HEAD_SIZE, GROUP * HEAD_SIZE), GROUP * HEAD_SIZE)
        return pltpu.make_async_copy(staged.at[:, part], result.at[:, part], sem.at[group])

    def fast(group, _):
        queries = all_queries(q_ref, query_marks, group)
        keys = all_keys(planes_of[-1], key_marks, tokens, group)
        values = all_values(planes_of[-1], tokens, group)
        weights = jnp.exp2(scores_of(queries, keys) * LOG2_SCALE).astype(jnp.bfloat16)
        summed = jnp.dot(weights, values, preferred_element_type=jnp.float32)
        here = pl.ds(pl.multiple_of(group * rows, rows), rows)
        if hops:
            summed = summed + running[here, :]
        if last:
            weight_sum = summed[:, HEAD_SIZE:]
            write(group, summed[:, :HEAD_SIZE] / weight_sum)
            sent(group).start()
            split = weight_sum.reshape(rows // 8, 8, HEAD_SIZE)
            least[...] = jnp.minimum(least[...], jnp.min(split, axis=0))
            most[...] = jnp.maximum(most[...], jnp.max(split, axis=0))
        else:
            result[here, :] = summed
        return 0

    lax.fori_loop(0, KEY_VALUE_HEADS, fast, 0)
    if not last:
        return
    for group in range(KEY_VALUE_HEADS):
        sent(group).wait()

    safe = (jnp.min(least[...]) >= SUM_LEAST) & (jnp.max(most[...]) <= SUM_MOST)

    @pl.when(jnp.logical_not(safe))
    def _():
        def careful(group, _):
            queries = all_queries(q_ref, query_marks, group)
            top = jnp.full((rows, 1), NEGATIVE_BIG, jnp.float32)
            total = jnp.zeros((rows, 2 * HEAD_SIZE), jnp.float32)
            for h in range(planes):
                mark_keys(doc_ref, key_marks, side, tokens, h)
                scores = scores_of(queries, all_keys(planes_of[h], key_marks, tokens, group)) * LOG2_SCALE
                new_top = jnp.maximum(top, jnp.max(scores, axis=1, keepdims=True))
                weights = jnp.exp2(scores - new_top).astype(jnp.bfloat16)
                total = total * jnp.exp2(top - new_top) + jnp.dot(
                    weights, all_values(planes_of[h], tokens, group), preferred_element_type=jnp.float32
                )
                top = new_top
            write(group, total[:, :HEAD_SIZE] / total[:, HEAD_SIZE:])
            sent(group).start()
            sent(group).wait()
            return 0

        lax.fori_loop(0, KEY_VALUE_HEADS, careful, 0)


def attend(doc_lengths, queries, planes, state, side, hops, last):
    tokens = queries.shape[0]
    rows = tokens * GROUP
    blocks = [b for plane in planes for b in plane]
    keys = len(planes[-1]) * tokens
    in_vmem = pl.BlockSpec(memory_space=pltpu.VMEM)
    kept = lambda value: pltpu.with_memory_space_constraint(value, pltpu.VMEM)
    operands = [kept(queries)] + [kept(b) for b in blocks] + ([] if state is None else [state])
    scratch = [pltpu.VMEM((keys, LANES), jnp.bfloat16), pltpu.VMEM((tokens, LANES), jnp.bfloat16)]
    if last:
        scratch += [
            pltpu.VMEM(queries.shape, queries.dtype),
            pltpu.VMEM((8, HEAD_SIZE), jnp.float32),
            pltpu.VMEM((8, HEAD_SIZE), jnp.float32),
            pltpu.SemaphoreType.DMA((KEY_VALUE_HEADS,)),
        ]
        out_shape, out_spec = jax.ShapeDtypeStruct(queries.shape, queries.dtype), pl.BlockSpec(memory_space=pl.ANY)
    else:
        out_shape = pltpu.VMEM((KEY_VALUE_HEADS * rows, 2 * HEAD_SIZE), jnp.float32)
        out_spec = in_vmem
    return pl.pallas_call(
        functools.partial(plane_kernel, side, hops, last),
        out_shape=out_shape,
        in_specs=[pl.BlockSpec(memory_space=pltpu.SMEM)] + [in_vmem] * len(operands),
        out_specs=out_spec,
        scratch_shapes=scratch,
        input_output_aliases={len(operands): 0} if hops and not last else {},
        name=f"plane_{hops}",
        cost_estimate=pl.CostEstimate(
            flops=8 * KEY_VALUE_HEADS * rows * keys * HEAD_SIZE,
            transcendentals=KEY_VALUE_HEADS * rows * keys,
            bytes_accessed=keys * 4096 + 4 * queries.size,
        ),
        compiler_params=pltpu.CompilerParams(vmem_limit_bytes=32 << 20),
    )(doc_lengths, *operands)


def on_device(sizes, token_queries, token_keys, token_values, doc_lengths):
    ctx, head = sizes
    side = head // CORES
    planes = ctx // side
    reach = planes // 2

    def shifted(dz, along):
        pairs = []
        for z in range(planes):
            for y in range(side):
                for x in range(side):
                    for core in range(CORES):
                        spot = [y, x]
                        if along is not None:
                            which = 1 - along if core == 0 else along
                            spot[which] = (spot[which] + 1) % side
                        up = (z + dz) % planes
                        pairs.append(
                            (((z * side + y) * side + x) * CORES + core, ((up * side + spot[0]) * side + spot[1]) * CORES + core)
                        )
        return pairs

    def send(value, dz=0, along=None):
        return lax.ppermute(value, AXES, shifted(dz, along))

    def partner(value):
        return lax.ppermute(value, "head", [(h, h ^ 1) for h in range(head)])

    def gathered(value):
        grid = [[None] * side for _ in range(side)]
        grid[0][0] = value
        for a in range(1, side):
            grid[a][0] = send(grid[a - 1][0], along=0)
        for a in range(side):
            for b in range(1, side):
                grid[a][b] = send(grid[a][b - 1], along=1)
        mine = [v for row in grid for v in row]
        return mine + [partner(v) for v in mine]

    layers = [jnp.concatenate([token_keys, token_values], axis=0)]
    for hop in range(reach):
        layers.append(send(layers[-1], dz=1))
    gathers = [gathered(layer) for layer in layers]
    state = None
    for hop in range(reach + 1):
        last = hop == reach
        state = attend(doc_lengths, token_queries, gathers if last else gathers[hop:hop + 1], state, side, hop, last)
    return state


def solution(mesh):
    spec = P(AXES, None)
    return jax.shard_map(
        functools.partial(on_device, (mesh.shape["ctx"], mesh.shape["head"])),
        mesh=mesh, in_specs=(spec, spec, spec, P()), out_specs=spec, check_vma=False,
    )
```

```python
import functools

import jax
import jax.numpy as jnp
import numpy as np
from jax import lax
from jax.experimental import pallas as pl
from jax.experimental.pallas import tpu as pltpu
from jax.sharding import PartitionSpec as P


QUERY_HEADS = 64
KEY_VALUE_HEADS = 8
HEAD_SIZE = 128
GROUP = QUERY_HEADS // KEY_VALUE_HEADS
CORES = 2
NEGATIVE_BIG = -1e30
LOG2_SCALE = HEAD_SIZE ** (-0.5) * float(np.log2(np.e))
SUM_LEAST, SUM_MOST = 2.0**-60, 2.0**100
FAR = 1 << 30
AXES = ("ctx", "head")
LANES = 128
IN_VMEM = pl.BlockSpec(memory_space=pltpu.VMEM)
ANYWHERE = pl.BlockSpec(memory_space=pl.ANY)
IN_HBM = pl.BlockSpec(memory_space=pltpu.HBM)
IN_SMEM = pl.BlockSpec(memory_space=pltpu.SMEM)
PARAMS = pltpu.CompilerParams(vmem_limit_bytes=16 << 20)


def columns(index):
    return pl.ds(pl.multiple_of(index * HEAD_SIZE, HEAD_SIZE), HEAD_SIZE)


def kept(value):
    return pltpu.with_memory_space_constraint(value, pltpu.VMEM)


def place(side):
    c, h = lax.axis_index("ctx"), lax.axis_index("head")
    return c // side, c % side, h // CORES, h % CORES


def block_base(side, tokens, label):
    hops, a, b, other_core = label
    z, y, x, core = place(side)
    own_base = (((z * side + y) * side + x) * CORES + core) * tokens
    on = core ^ other_core
    dx, dy = jnp.where(on == 0, a, b), jnp.where(on == 0, b, a)
    from_x, from_y = lax.rem(x - dx + side, side), lax.rem(y - dy + side, side)
    base = ((((z - hops) * side + from_y) * side + from_x) * CORES + on) * tokens
    return jnp.where((z >= hops) & (base <= own_base), base, -(FAR >> 1))


def prepare_kernel(side, labels, doc_ref, q_ref, kept_ref, query_marks, *refs):
    *key_marks, sem = refs
    copy = pltpu.make_async_copy(q_ref, kept_ref, sem)
    copy.start()
    tokens = q_ref.shape[0]
    tail = LANES - tokens
    lane = lax.broadcasted_iota(jnp.int32, (1, LANES), 1)
    low, high = jnp.where(lane >= tail, -FAR, 0), jnp.where(lane >= tail, FAR, 0)
    start = jnp.int32(0)
    for d in range(doc_ref.shape[0]):
        stop = start + doc_ref[d]
        low, high = jnp.where(lane == d, start, low), jnp.where(lane == d, stop, high)
        start = stop
    inside = lax.broadcasted_iota(jnp.int32, (tokens, LANES), 0)
    lane = lax.broadcasted_iota(jnp.int32, (tokens, LANES), 1)
    position = block_base(side, tokens, (0, 0, 0, 0)) + inside
    one = (lane - tail == inside) | ((position >= low) & (position < high) & (lane < tail))
    query_marks[...] = jnp.where(one, 1.0, 0.0).astype(query_marks.dtype)
    for marks, stage in zip(key_marks, labels):
        for index, label in enumerate(stage):
            position = block_base(side, tokens, label) + inside
            hidden = (position < low) | (position >= high)
            if label == (0, 0, 0, 0):
                hidden |= (lane >= tail) & (lane - tail < inside)
            marks[index * tokens:(index + 1) * tokens, :] = jnp.where(hidden, NEGATIVE_BIG, 0.0).astype(marks.dtype)
    copy.wait()


def prepare(doc_lengths, queries, side, labels):
    tokens = queries.shape[0]
    marks = lambda count: pltpu.VMEM((count * tokens, LANES), jnp.bfloat16)
    q, query_marks, *key_marks = pl.pallas_call(
        functools.partial(prepare_kernel, side, labels),
        out_shape=[pltpu.VMEM(queries.shape, queries.dtype), marks(1)] + [marks(len(stage)) for stage in labels],
        in_specs=[IN_SMEM, IN_HBM],
        out_specs=[IN_VMEM] * (2 + len(labels)),
        scratch_shapes=[pltpu.SemaphoreType.DMA],
        compiler_params=PARAMS,
        name="prepare",
    )(
        pltpu.with_memory_space_constraint(doc_lengths, pltpu.SMEM),
        pltpu.with_memory_space_constraint(queries, pltpu.HBM),
    )
    return q, query_marks, key_marks


def begin_kernel(plane_tokens, doc_hbm, keys_ref, values_ref, own_ref, spanned_ref, lengths_ref, doc_ref, sem):
    tokens = keys_ref.shape[0]
    lengths = pltpu.make_async_copy(doc_hbm, doc_ref, sem.at[2])
    lengths.start()
    copies = [
        pltpu.make_async_copy(keys_ref, own_ref.at[:tokens, :], sem.at[0]),
        pltpu.make_async_copy(values_ref, own_ref.at[tokens:, :], sem.at[1]),
    ]
    for copy in copies:
        copy.start()
    lengths.wait()
    start, most = jnp.int32(0), jnp.int32(0)
    for d in range(doc_ref.shape[0]):
        lengths_ref[d] = doc_ref[d]
        stop = start + doc_ref[d]
        most = jnp.maximum(most, lax.div(stop - 1, plane_tokens) - lax.div(start, plane_tokens))
        start = stop
    spanned_ref[0] = most
    for copy in copies:
        copy.wait()


def begin(doc_lengths, keys, values, plane_tokens):
    hbm = lambda a: pltpu.with_memory_space_constraint(a, pltpu.HBM)
    return pl.pallas_call(
        functools.partial(begin_kernel, plane_tokens),
        out_shape=(pltpu.VMEM((2 * keys.shape[0], keys.shape[1]), keys.dtype), pltpu.SMEM((1,), jnp.int32),
                   pltpu.SMEM(doc_lengths.shape, jnp.int32)),
        in_specs=[IN_HBM] * 3,
        out_specs=(IN_VMEM, IN_SMEM, IN_SMEM),
        scratch_shapes=[pltpu.SMEM(doc_lengths.shape, jnp.int32), pltpu.SemaphoreType.DMA((3,))],
        compiler_params=PARAMS,
        name="begin",
    )(hbm(doc_lengths), hbm(keys), hbm(values))


def all_queries(q_ref, marks_ref, group):
    marks = marks_ref[...]
    return jnp.concatenate(
        [jnp.concatenate([q_ref[:, columns(group * GROUP + r)], marks], axis=1) for r in range(GROUP)], axis=0
    )


def stage_parts(refs, marks, tokens, group):
    spots = [(ref, at) for ref in refs for at in range(0, ref.shape[0], 2 * tokens)]
    keys = jnp.concatenate([ref[at:at + tokens, columns(group)] for ref, at in spots], axis=0)
    values = jnp.concatenate([ref[at + tokens:at + 2 * tokens, columns(group)] for ref, at in spots], axis=0)
    return jnp.concatenate([keys, marks[...]], axis=1), jnp.concatenate([values, jnp.ones_like(values)], axis=1)


def scaled_scores(queries, keys):
    return LOG2_SCALE * lax.dot_general(
        queries, keys, (((1,), (1,)), ((), ())), preferred_element_type=jnp.float32
    )


def stage_kernel(counts, first, last, q_ref, query_marks, *refs):
    tokens = q_ref.shape[0]
    rows = tokens * GROUP
    stages = []
    for count in counts:
        stages.append((refs[1:count + 1], refs[0]))
        refs = refs[count + 1:]
    if not first:
        running, refs = refs[0], refs[1:]
    if last:
        result, staged, least, most, sem = refs
        least[...] = jnp.full(least.shape, SUM_MOST, jnp.float32)
        most[...] = jnp.full(most.shape, SUM_LEAST, jnp.float32)
    else:
        (result,) = refs

    def write(group, mean):
        for r in range(GROUP):
            staged[:, columns(group * GROUP + r)] = mean[r * tokens:(r + 1) * tokens].astype(staged.dtype)

    def sent(group):
        part = pl.ds(pl.multiple_of(group * GROUP * HEAD_SIZE, GROUP * HEAD_SIZE), GROUP * HEAD_SIZE)
        return pltpu.make_async_copy(staged.at[:, part], result.at[:, part], sem.at[group])

    def fast(group, _):
        keys, values = stage_parts(*stages[-1], tokens, group)
        weights = jnp.exp2(scaled_scores(all_queries(q_ref, query_marks, group), keys)).astype(jnp.bfloat16)
        summed = jnp.dot(weights, values, preferred_element_type=jnp.float32)
        here = pl.ds(pl.multiple_of(group * rows, rows), rows)
        if not first:
            summed = summed + running[here, :]
        if last:
            weight_sum = summed[:, HEAD_SIZE:]
            write(group, summed[:, :HEAD_SIZE] * pl.reciprocal(weight_sum))
            sent(group).start()
            split = weight_sum.reshape(rows // 8, 8, HEAD_SIZE)
            least[...] = jnp.minimum(least[...], jnp.min(split, axis=0))
            most[...] = jnp.maximum(most[...], jnp.max(split, axis=0))
        else:
            result[here, :] = summed
        return 0

    lax.fori_loop(0, KEY_VALUE_HEADS, fast, 0, unroll=4)
    if not last:
        return
    for group in range(KEY_VALUE_HEADS):
        sent(group).wait()
    safe = (jnp.min(least[...]) >= SUM_LEAST) & (jnp.max(most[...]) <= SUM_MOST)

    @pl.when(jnp.logical_not(safe))
    def _():
        def careful(group, _):
            queries = all_queries(q_ref, query_marks, group)
            top = jnp.full((rows, 1), NEGATIVE_BIG, jnp.float32)
            total = jnp.zeros((rows, 2 * HEAD_SIZE), jnp.float32)
            for arrays, marks in stages:
                keys, values = stage_parts(arrays, marks, tokens, group)
                scores = scaled_scores(queries, keys)
                new_top = jnp.maximum(top, jnp.max(scores, axis=1, keepdims=True))
                weights = jnp.exp2(scores - new_top).astype(jnp.bfloat16)
                total = total * jnp.exp2(top - new_top) + jnp.dot(weights, values, preferred_element_type=jnp.float32)
                top = new_top
            write(group, total[:, :HEAD_SIZE] / total[:, HEAD_SIZE:])
            sent(group).start()
            sent(group).wait()
            return 0

        lax.fori_loop(0, KEY_VALUE_HEADS, careful, 0)


def attend(q, query_marks, stages, state, last):
    tokens = q.shape[0]
    rows = tokens * GROUP
    stages = stages if last else stages[-1:]
    operands = [kept(q), kept(query_marks)]
    for marks, arrays in stages:
        operands += [kept(marks)] + [kept(a) for a in arrays]
    if state is not None:
        operands.append(kept(state))
    scratch = []
    if last:
        scratch = [
            pltpu.VMEM(q.shape, q.dtype),
            pltpu.VMEM((8, HEAD_SIZE), jnp.float32),
            pltpu.VMEM((8, HEAD_SIZE), jnp.float32),
            pltpu.SemaphoreType.DMA((KEY_VALUE_HEADS,)),
        ]
        out_shape, out_spec = pltpu.HBM(q.shape, q.dtype), IN_HBM
    else:
        out_shape, out_spec = pltpu.VMEM((KEY_VALUE_HEADS * rows, 2 * HEAD_SIZE), jnp.float32), IN_VMEM
    keys = stages[-1][0].shape[0]
    return pl.pallas_call(
        functools.partial(stage_kernel, [len(arrays) for _, arrays in stages], state is None, last),
        out_shape=out_shape,
        in_specs=[IN_VMEM] * len(operands),
        out_specs=out_spec,
        scratch_shapes=scratch,
        input_output_aliases={} if last or state is None else {len(operands) - 1: 0},
        cost_estimate=pl.CostEstimate(
            flops=8 * KEY_VALUE_HEADS * rows * keys * HEAD_SIZE,
            transcendentals=KEY_VALUE_HEADS * rows * keys,
            bytes_accessed=keys * 4096 + 4 * q.size,
        ),
        compiler_params=PARAMS,
    )(*operands)


def after(value, *others):
    return lax.optimization_barrier((value, *others))


def on_device(sizes, token_queries, token_keys, token_values, doc_lengths):
    ctx, head = sizes
    side = head // CORES
    reach = ctx // side // 2
    own, spanned, lengths = begin(doc_lengths, token_keys, token_values, token_queries.shape[0] * CORES * side * side)
    return lax.cond(
        spanned[0] >= reach,
        functools.partial(with_reach, ctx, head, reach),
        functools.partial(with_reach, ctx, head, reach - 1),
        token_queries, own, lengths,
    )


def with_reach(ctx, head, reach, *arrays):
    return gather_and_attend(ctx, head, reach, *arrays)


def gather_and_attend(ctx, head, reach, token_queries, own, doc_lengths):
    side = head // CORES
    planes = ctx // side

    def shifted(dz, along):
        pairs = []
        for z in range(planes):
            for y in range(side):
                for x in range(side):
                    for core in range(CORES):
                        spot = [y, x]
                        if along is not None:
                            which = 1 - along if core == 0 else along
                            spot[which] = (spot[which] + 1) % side
                        up = (z + dz) % planes
                        pairs.append(
                            (((z * side + y) * side + x) * CORES + core, ((up * side + spot[0]) * side + spot[1]) * CORES + core)
                        )
        return pairs

    def send(value, dz=0, along=None):
        return lax.ppermute(value, AXES, shifted(dz, along))

    def partner(value):
        return lax.ppermute(value, "head", [(h, h ^ 1) for h in range(head)])

    starts, rounds, _ = plan(side, reach)
    labels = [[(*spot, s) for s in range(CORES) for spot in blocks] for blocks in rounds]
    q, query_marks, key_marks = prepare(doc_lengths, token_queries, side, labels)
    grid = {(0, 0, 0): own}
    states, stages = [None], []

    def attend_round():
        spots = rounds[len(stages)]
        for spot in spots:
            if spot not in pairs:
                pairs[spot] = partner(grid[spot])
        marks = key_marks[len(stages)]
        stages.append((marks, [grid[spot] for spot in spots] + [pairs[spot] for spot in spots]))
        last = len(stages) == len(rounds)
        states.append(attend(q, query_marks, stages, states[-1], last))

    pairs = {(0, 0, 0): partner(own)}
    for spot in starts:
        hops, a, b = spot
        if len(stages) + 2 < len(rounds) and spot == sorted(rounds[len(stages) + 2], key=starts.index)[-2]:
            attend_round()
            held = states[-1]
        else:
            held = None
        if a == 0 and hops:
            source, move = (hops - 1, a, b), dict(dz=1)
        elif b:
            source, move = (hops, a, b - 1), dict(along=1)
        else:
            source, move = (hops, a - 1, b), dict(along=0)
        value = grid[source]
        if held is not None:
            value, states[-1] = after(value, held)
        grid[spot] = send(value, **move)
        if spot == (1, 0, 0):
            grid[spot], q, query_marks, *key_marks = after(grid[spot], q, query_marks, *key_marks)
    while len(stages) + 1 < len(rounds):
        attend_round()
    for spot in starts[-2:]:
        grid[spot], states[-1] = after(grid[spot], states[-1])
    attend_round()
    return states[-1]


def plan(side, reach):
    spots = [(h, a, b) for h in range(reach + 1) for a in range(side) for b in range(side)]

    def arrival(spot):
        hops, a, b = spot
        return 2 * hops + a + b + (a > 0 and b > 0), -hops, b

    def start(spot):
        hops, a, b = spot
        if spot == (1, 0, 0):
            return 0, 0, 0
        if a == b == 0:
            return 2 * hops - 1.5, -hops, 0
        late = 0.1 * (a > 0 and b > 0) + 0.2 * (a > 0 and b == 0 and hops == reach > 1) + 0.5 * (a == 0 and hops > 0)
        return 2 * hops + a + b + (a > 0 and b > 0) + late, -hops, b

    size = side * side
    ordered = sorted(spots, key=arrival)
    rounds = [ordered[i:i + size] for i in range(0, len(ordered), size)]
    starts = sorted(spots[1:], key=start)
    gates = [starts[min(map(starts.index, r)) - 1] for r in rounds[2:]] + [starts[-2], starts[-1]]
    gates = gates[-len(rounds):]
    return starts, rounds, gates


def solution(mesh):
    spec = P(AXES, None)
    sizes = mesh.shape["ctx"], mesh.shape["head"]
    return jax.shard_map(
        functools.partial(on_device, sizes), mesh=mesh, in_specs=(spec, spec, spec, P()), out_specs=spec, check_vma=False
    )
```
